128 devices in a mesh: pipe: 4 (over y), tensor: 32 (over z, x, core).
Axes of the slice: x: 4, y: 4, z: 4, core: 2. Of those that a mesh axis runs over, the one named last changes fastest.
Arguments:
- inputs: bfloat16 [8, 128, 8192], P(None, None, 'tensor'), may hold values from -60 to 60
- cotangent: bfloat16 [8, 128, 8192], P(None, None, 'tensor'), may hold values from -13 to 13
- norm_gain: float32 [4, 8192], P('pipe', 'tensor'), may hold values from 0.25 to 1.75
- first_factor: bfloat16 [4, 64, 128, 512], P('pipe', 'tensor'), may hold values from -0.35355339 to 0.35355339
- second_factor: bfloat16 [4, 128, 256, 256], P('pipe', 'tensor'), may hold values from -0.25 to 0.25
- third_factor: bfloat16 [4, 128, 256, 256], P('pipe', 'tensor'), may hold values from -0.3125 to 0.3125
- fourth_factor: bfloat16 [4, 64, 512, 128], P('pipe', 'tensor'), may hold values from -0.22097087 to 0.22097087
Outputs:
- section_out: bfloat16 [4, 8, 128, 8192], P('pipe', None, None, 'tensor')
- section_grad: bfloat16 [4, 8, 128, 8192], P('pipe', None, None, 'tensor')
- gain_grad: float32 [4, 8192], P('pipe', 'tensor')
- first_grad: float32 [4, 64, 128, 512], P('pipe', 'tensor')
- second_grad: float32 [4, 128, 256, 256], P('pipe', 'tensor')
- third_grad: float32 [4, 128, 256, 256], P('pipe', 'tensor')
- fourth_grad: float32 [4, 64, 512, 128], P('pipe', 'tensor')
The draws below stay inside these ranges and needn't reach their ends.
All inputs are finite; a program needn't handle non-finite values.
Results may differ from the reference program's by a relative error of at most 0.013.
Values may be sent and summed in bfloat16 or wider, within the bound.
No kernel may reach another device: no remote copies, remote signals or barrier semaphores. Data moves between devices by JAX's collectives and lax.ppermute only.
A program may use at most 128 MiB of HBM per device.

```python
import math
import jax
import jax.numpy as jnp
from jax import lax

D = 8192
BLK = 128
TOK = 128
MICRO = 8
NB = 64
EXPAND = 4
Q = 256
SECTIONS = 4


def stream_parts(key):
    key_base = jax.random.fold_in(key, 11)
    key_groups = jax.random.fold_in(key, 12)
    key_rows = jax.random.fold_in(key, 13)
    groups = NB // 2
    group_scale = jnp.power(10.0, jax.random.uniform(key_groups, (MICRO, TOK, groups, 1), jnp.float32, -0.75, 0.75))
    row_scale = jnp.power(10.0, jax.random.uniform(key_rows, (MICRO, TOK, 1, 1), jnp.float32) - 0.5)
    base = jnp.clip(jax.random.normal(key_base, (MICRO, TOK, groups, 2 * BLK), jnp.float32), -3.0, 3.0)
    return (base, group_scale, row_scale)


def draw_inputs(key, part):
    base, group_scale, row_scale = stream_parts(key)
    return (base * group_scale * row_scale).reshape(MICRO, TOK, D).astype(jnp.bfloat16)


def draw_cotangent(key, part):
    base, group_scale, row_scale = stream_parts(key)
    key_noise = jax.random.fold_in(key, 14)
    noise = jnp.clip(jax.random.normal(key_noise, (MICRO, TOK, D), jnp.float32), -4.0, 4.0)
    shared = (0.5 * base * group_scale).reshape(MICRO, TOK, D)
    return (shared + noise).astype(jnp.bfloat16)


def clipped_normal(key, shape):
    return jnp.clip(jax.random.normal(key, shape, jnp.float32), -3.0, 3.0)


def outer_base(key):
    return clipped_normal(jax.random.fold_in(key, 21), (SECTIONS, NB, BLK, EXPAND * BLK))


def middle_base(key):
    return clipped_normal(jax.random.fold_in(key, 31), (SECTIONS, BLK, Q, Q))


def draw_first_factor(key, part):
    return (outer_base(key) * BLK ** (-0.5)).astype(jnp.bfloat16)


def draw_fourth_factor(key, part):
    tied = jnp.swapaxes(outer_base(key), 2, 3)
    fresh = clipped_normal(jax.random.fold_in(key, 22), (SECTIONS, NB, EXPAND * BLK, BLK))
    return ((0.8 * tied + 0.6 * fresh) * (EXPAND * BLK) ** (-0.5)).astype(jnp.bfloat16)


def draw_second_factor(key, part):
    return (middle_base(key) * Q ** (-0.5)).astype(jnp.bfloat16)


def draw_third_factor(key, part):
    tied = jnp.swapaxes(middle_base(key), 2, 3)
    fresh = clipped_normal(jax.random.fold_in(key, 32), (SECTIONS, BLK, Q, Q))
    return ((0.8 * tied + 0.6 * fresh) * Q ** (-0.5)).astype(jnp.bfloat16)


def setup_inputs(seed: int = 0) -> dict:
    streams_of = jax.random.split(jax.random.key(seed), 8)
    return {
        "inputs": draw_inputs(jax.random.fold_in(streams_of[7], 71), 0),
        "cotangent": draw_cotangent(jax.random.fold_in(streams_of[7], 71), 0),
        "norm_gain": jnp.clip(1.0 + 0.15 * jax.random.normal(streams_of[2], (SECTIONS, D), jnp.float32), 0.25, 1.75),
        "first_factor": draw_first_factor(jax.random.fold_in(streams_of[7], 71), 0),
        "second_factor": draw_second_factor(jax.random.fold_in(streams_of[7], 71), 0),
        "third_factor": draw_third_factor(jax.random.fold_in(streams_of[7], 71), 0),
        "fourth_factor": draw_fourth_factor(jax.random.fold_in(streams_of[7], 71), 0),
    }


EPS = 1e-05
TANH_SCALE = math.sqrt(2.0 / math.pi)
CUBIC_COEF = 0.044715

def gelu_pair(preact):
    tanh_val = jnp.tanh(TANH_SCALE * (preact + CUBIC_COEF * preact * preact * preact))
    gelu_value = 0.5 * preact * (1.0 + tanh_val)
    gelu_slope = 0.5 * (1.0 + tanh_val) + 0.5 * preact * (1.0 - tanh_val * tanh_val) * TANH_SCALE * (1.0 + 3.0 * CUBIC_COEF * preact * preact)
    return (gelu_value, gelu_slope)

def as_float(values):
    return values.astype(jnp.float32)

def factors_of(first_w, second_w, third_w, fourth_w):
    return (as_float(first_w.reshape(NB, BLK, EXPAND, BLK)), as_float(second_w.reshape(BLK, NB, EXPAND, Q)), as_float(third_w.reshape(BLK, Q, NB, EXPAND)), as_float(fourth_w.reshape(NB, EXPAND, BLK, BLK)))

def forward_section(stream_in, gain_row, factors):
    factor_one, factor_two, factor_three, factor_four = factors
    stream = as_float(stream_in)
    inv_rms = lax.rsqrt(lax.optimization_barrier(jnp.mean(stream * stream, axis=-1, keepdims=True)) + EPS)
    normed = (stream * inv_rms * gain_row).astype(jnp.bfloat16)
    spread = jnp.einsum('tij,ijak->tiak', as_float(normed.reshape(TOK, NB, BLK)), factor_one).astype(jnp.bfloat16)
    preact = jnp.einsum('tiac,ciae->tce', as_float(spread), factor_two)
    gelu_value, gelu_slope = gelu_pair(preact)
    activated = gelu_value.astype(jnp.bfloat16)
    mixed = jnp.einsum('tce,ceia->tiac', as_float(activated), factor_three).astype(jnp.bfloat16)
    branch = jnp.einsum('tiak,iakj->tij', as_float(mixed), factor_four).reshape(TOK, D)
    result = (stream + branch).astype(jnp.bfloat16)
    return (result, (stream, inv_rms, normed, spread, activated, gelu_slope, mixed))

def backward_section(grad_out, record, gain_row, factors):
    factor_one, factor_two, factor_three, factor_four = factors
    stream, inv_rms, normed, spread, activated, gelu_slope, mixed = record
    grad_blocks = as_float(grad_out.reshape(TOK, NB, BLK))
    part_four = jnp.einsum('tiak,tij->iakj', as_float(mixed), grad_blocks)
    grad_mixed = jnp.einsum('tij,iakj->tiak', grad_blocks, factor_four).astype(jnp.bfloat16)
    part_three = jnp.einsum('tce,tiac->ceia', as_float(activated), as_float(grad_mixed))
    grad_act = jnp.einsum('tiac,ceia->tce', as_float(grad_mixed), factor_three)
    grad_pre = (grad_act * gelu_slope).astype(jnp.bfloat16)
    part_two = jnp.einsum('tiac,tce->ciae', as_float(spread), as_float(grad_pre))
    grad_spread = jnp.einsum('tce,ciae->tiac', as_float(grad_pre), factor_two).astype(jnp.bfloat16)
    part_one = jnp.einsum('tij,tiak->ijak', as_float(normed.reshape(TOK, NB, BLK)), as_float(grad_spread))
    grad_norm = jnp.einsum('tiak,ijak->tij', as_float(grad_spread), factor_one).reshape(TOK, D)
    part_gain = lax.optimization_barrier(jnp.sum(grad_norm * stream * inv_rms, axis=0))
    scaled_grad = grad_norm * gain_row
    inner_sum = lax.optimization_barrier(jnp.sum(scaled_grad * stream, axis=-1, keepdims=True))
    grad_in = (as_float(grad_out) + scaled_grad * inv_rms - stream * inv_rms * inv_rms * inv_rms * inner_sum / D).astype(jnp.bfloat16)
    parts = (part_gain, part_one.reshape(NB, BLK, EXPAND * BLK), part_two.reshape(BLK, Q, Q), part_three.reshape(BLK, Q, Q), part_four.reshape(NB, EXPAND * BLK, BLK))
    return (grad_in, parts)

def reference(inputs, cotangent, norm_gain, first_factor, second_factor, third_factor, fourth_factor):
    outs_list = [[None] * MICRO for section_id in range(SECTIONS)]
    grads_list = [[None] * MICRO for section_id in range(SECTIONS)]
    totals = [[jnp.zeros((D,), jnp.float32), jnp.zeros((NB, BLK, EXPAND * BLK), jnp.float32), jnp.zeros((BLK, Q, Q), jnp.float32), jnp.zeros((BLK, Q, Q), jnp.float32), jnp.zeros((NB, EXPAND * BLK, BLK), jnp.float32)] for section_id in range(SECTIONS)]
    for micro_id in range(MICRO):
        stream_in = inputs[micro_id]
        records = []
        for section_id in range(SECTIONS):
            factors = factors_of(first_factor[section_id], second_factor[section_id], third_factor[section_id], fourth_factor[section_id])
            result, record = forward_section(stream_in, norm_gain[section_id], factors)
            outs_list[section_id][micro_id] = result
            records.append(record)
            stream_in = result
        grad_out = cotangent[micro_id]
        for section_id in reversed(range(SECTIONS)):
            factors = factors_of(first_factor[section_id], second_factor[section_id], third_factor[section_id], fourth_factor[section_id])
            grad_in, parts = backward_section(grad_out, records[section_id], norm_gain[section_id], factors)
            grads_list[section_id][micro_id] = grad_in
            totals[section_id] = [total + member for total, member in zip(totals[section_id], parts)]
            grad_out = grad_in
    section_out = jnp.stack([jnp.stack(row) for row in outs_list])
    section_grad = jnp.stack([jnp.stack(row) for row in grads_list])
    gain_grad = jnp.stack([totals[section_id][0] for section_id in range(SECTIONS)])
    first_grad = jnp.stack([totals[section_id][1] for section_id in range(SECTIONS)])
    second_grad = jnp.stack([totals[section_id][2] for section_id in range(SECTIONS)])
    third_grad = jnp.stack([totals[section_id][3] for section_id in range(SECTIONS)])
    fourth_grad = jnp.stack([totals[section_id][4] for section_id in range(SECTIONS)])
    return (section_out, section_grad, gain_grad, first_grad, second_grad, third_grad, fourth_grad)
```

```python
import functools
import math

import jax
import jax.numpy as jnp
from jax import lax
from jax.experimental import pallas as pl
from jax.experimental.pallas import tpu as pltpu
from jax.sharding import PartitionSpec as P

EPS = 1e-05
TANH_SCALE = math.sqrt(2.0 / math.pi)
CUBIC_COEF = 0.044715
F32, BF16 = jnp.float32, jnp.bfloat16

ROWS_MID, ROWS_OUT = 2048, 512


def dot(lhs, rhs, contract):
    return lax.dot_general(lhs, rhs, ((contract[:1], contract[1:]), ((), ())), preferred_element_type=F32)


def nn(lhs, rhs):
    return dot(lhs, rhs, (1, 0))


def tn(lhs, rhs):
    return dot(lhs, rhs, (0, 0))


def nt(lhs, rhs):
    return dot(lhs, rhs, (1, 1))


def one_hot(hit):
    return jnp.where(hit, 1.0, 0.0).astype(BF16)


def iotas():
    return lax.broadcasted_iota(jnp.int32, (256, 256), 0), lax.broadcasted_iota(jnp.int32, (256, 256), 1)


def feature_pack():
    out, inn = iotas()
    return one_hot(inn == (out & 3) * 64 + (out >> 2))


def feature_unpack():
    out, inn = iotas()
    return one_hot(out == (inn & 3) * 64 + (inn >> 2))


def hidden_unpack():
    out, inn = iotas()
    return one_hot(inn == ((out & 63) >> 2) * 16 + (out >> 6) * 4 + (out & 3))


def hidden_pack():
    out, inn = iotas()
    return one_hot(out == ((inn & 63) >> 2) * 16 + (inn >> 6) * 4 + (inn & 3))


def lanes(parts):
    return jnp.concatenate(parts, axis=1)


def rows(parts):
    return jnp.concatenate(parts, axis=0)


def send_features(out_ref, base, values):
    pack = feature_pack()
    for i in range(2):
        part = values[i].astype(BF16)
        for group in range(2):
            picked = rows([part[a * 128 + group * 64 : a * 128 + group * 64 + 64] for a in range(4)])
            packed = nn(pack, picked).astype(BF16)
            for half in range(2):
                start = base + half * 32 + i * 16
                out_ref[group * 16 : group * 16 + 16, start : start + 16, :] = packed[
                    :, half * 128 : half * 128 + 128
                ].reshape(16, 16, 128)


def take_features(in_ref, base):
    unpack = feature_unpack()
    blocks = []
    for i in range(2):
        groups = []
        for group in range(2):
            halves = []
            for half in range(2):
                start = base + half * 32 + i * 16
                halves.append(in_ref[group * 16 : group * 16 + 16, start : start + 16, :].reshape(256, 128))
            groups.append(nn(unpack, lanes(halves)).astype(BF16))
        blocks.append(rows([groups[g][a * 64 : a * 64 + 64] for a in range(4) for g in range(2)]))
    return blocks


def send_hidden(out_ref, base, values):
    pack = hidden_pack()
    for group in range(4):
        picked = rows([values[c][group * 64 : group * 64 + 64] for c in range(4)])
        packed = nn(pack, picked).astype(BF16)
        for half in range(2):
            start = base + half * 32
            out_ref[group * 8 : group * 8 + 8, start : start + 32, :] = packed[
                :, half * 128 : half * 128 + 128
            ].reshape(8, 32, 128)


def take_hidden(in_ref, base):
    unpack = hidden_unpack()
    groups = []
    for group in range(4):
        halves = []
        for half in range(2):
            start = base + half * 32
            halves.append(in_ref[group * 8 : group * 8 + 8, start : start + 32, :].reshape(256, 128))
        groups.append(nn(unpack, lanes(halves)).astype(BF16))
    return [rows([groups[g][c * 64 : c * 64 + 64] for g in range(4)]) for c in range(4)]


def send_total(out_ref, base, total):
    high = total.astype(BF16).astype(F32)
    low = total - high
    block = rows(
        [high[:, :128], high[:, 128:], low[:, :128], low[:, 128:], jnp.zeros((4, 128), F32)]
    ).astype(BF16)
    out_ref[:, base : base + 8, :] = jnp.broadcast_to(block[None], (32, 8, 128))


def take_total(in_ref, base):
    summed = jnp.sum(in_ref[:, base : base + 8, :].astype(F32), axis=0)
    return lanes([summed[0:1] + summed[2:3], summed[1:2] + summed[3:4]])


def gelu_pair(preact):
    tanh_val = jnp.tanh(TANH_SCALE * (preact + CUBIC_COEF * preact * preact * preact))
    gelu_value = 0.5 * preact * (1.0 + tanh_val)
    gelu_slope = 0.5 * (1.0 + tanh_val) + 0.5 * preact * (
        1.0 - tanh_val * tanh_val
    ) * TANH_SCALE * (1.0 + 3.0 * CUBIC_COEF * preact * preact)
    return (gelu_value, gelu_slope)


def gain_column(gain_ref):
    row = gain_ref[0, 0:1, :].astype(F32) + gain_ref[0, 1:2, :].astype(F32) + gain_ref[0, 2:3, :].astype(F32)
    cols = []
    for i in range(2):
        square = jnp.broadcast_to(row[:, i * 128 : i * 128 + 128], (128, 128)).T
        cols.append(lanes([square, square]))
    return rows(cols)


def first_of(first_ref, i):
    return lanes([first_ref[0, h * 256 + i * 128 : h * 256 + i * 128 + 128, :] for h in range(2)])


def fourth_of(fourth_ref, i):
    return fourth_ref[0, :, i * 128 : i * 128 + 128]


def enter_layer(stream, gain_ref, first_ref, wire_ref):
    send_total(wire_ref, 64, jnp.sum(stream * stream, axis=0, keepdims=True))
    scaled = (stream * gain_column(gain_ref)).astype(BF16)
    send_features(
        wire_ref, 0, [tn(first_of(first_ref, i), scaled[i * 128 : i * 128 + 128]) for i in range(2)]
    )


def leave_layer(stream, mixed, fourth_ref):
    branch = rows([tn(fourth_of(fourth_ref, i), mixed[i]) for i in range(2)])
    return (stream + branch).astype(BF16)


def pack_kernel(first_ref, second_ref, third_ref, fourth_ref, gain_ref, out_ref):
    for copy in range(4):
        for c in range(4):
            out_ref[copy, c * 256 : c * 256 + 256, :] = second_ref[0, c]
            out_ref[copy, 1024 + c * 256 : 1024 + c * 256 + 256, :] = third_ref[0, c]
        for i in range(2):
            for h in range(2):
                start = ROWS_MID + h * 256 + i * 128
                out_ref[copy, start : start + 128, :] = first_ref[0, i, :, h * 256 : h * 256 + 256]
        start = ROWS_MID + ROWS_OUT
        out_ref[copy, start : start + ROWS_OUT, :] = lanes([fourth_ref[0, 0], fourth_ref[0, 1]])
        gain = gain_ref[...]
        high = gain.astype(BF16).astype(F32)
        mid = (gain - high).astype(BF16).astype(F32)
        low = gain - high - mid
        out_ref[copy, start + ROWS_OUT : start + ROWS_OUT + 16, :] = rows(
            [high, mid, low, jnp.zeros((13, 256), F32)]
        ).astype(BF16)


def start_kernel(slot_ref, input_ref, first_ref, gain_ref, wire_ref, stream_ref):
    stream = input_ref[...].astype(F32).reshape(256, 256).T
    stream_ref[...] = stream.astype(BF16)
    enter_layer(stream, gain_ref, first_ref, wire_ref)


def inv_rms_of(wire_ref):
    return lax.rsqrt(take_total(wire_ref, 64) / 8192.0 + EPS)


def hidden_forward_kernel(wire_ref, middle_ref, out_ref, spread_ref, preact_ref, act_ref, inv_ref):
    inv_rms = inv_rms_of(wire_ref)
    inv_ref[...] = jnp.broadcast_to(inv_rms, (8, 256))
    spread = take_hidden(wire_ref, 0)
    mixed = []
    for c in range(4):
        spread_ref[c] = spread[c]
        preact = tn(middle_ref[0, c * 256 : c * 256 + 256, :], spread[c]) * inv_rms
        preact_ref[c] = preact
        tanh_val = jnp.tanh(TANH_SCALE * (preact + CUBIC_COEF * preact * preact * preact))
        act = (0.5 * preact * (1.0 + tanh_val)).astype(BF16)
        act_ref[c] = act
        mixed.append(tn(middle_ref[0, 1024 + c * 256 : 1024 + c * 256 + 256, :], act).astype(BF16))
    send_hidden(out_ref, 0, mixed)


def between_kernel(wire_ref, stream_ref, fourth_ref, first_ref, gain_ref, out_ref, next_ref, mixed_ref, section_ref):
    mixed = take_features(wire_ref, 0)
    mixed_ref[0], mixed_ref[1] = mixed[0], mixed[1]
    result = leave_layer(stream_ref[...].astype(F32), mixed, fourth_ref)
    next_ref[...] = result
    stream = result.astype(F32)
    enter_layer(stream, gain_ref, first_ref, out_ref)
    section_ref[...] = stream.T.astype(BF16)


def turn_kernel(
    slot_ref, wire_ref, stream_ref, fourth_ref, first_ref, gain_ref, cotangent_ref, last_fourth_ref,
    out_ref, next_ref, mixed_ref, section_ref, grad_ref,
):
    between_kernel(
        wire_ref, stream_ref, fourth_ref, first_ref, gain_ref, out_ref, next_ref, mixed_ref, section_ref
    )
    grad = cotangent_ref[...].astype(F32).reshape(256, 256).T.astype(BF16)
    grad_ref[...] = grad
    send_grad(out_ref, 72, grad, last_fourth_ref)


def send_grad(out_ref, base, grad, fourth_ref):
    send_features(
        out_ref, base, [nn(fourth_of(fourth_ref, i), grad[i * 128 : i * 128 + 128]) for i in range(2)]
    )


def hidden_backward(c, grad_mixed, act, preact, slope, inv_rms, spread, middle_ref, grads_ref):
    grads_ref[1024 + c * 256 : 1024 + c * 256 + 256, :] = nt(act, grad_mixed).astype(BF16)
    grad_act = nn(middle_ref[0, 1024 + c * 256 : 1024 + c * 256 + 256, :], grad_mixed)
    grad_pre = grad_act * slope * inv_rms
    part = jnp.sum(grad_pre * preact, axis=0, keepdims=True)
    grad_pre = grad_pre.astype(BF16)
    grads_ref[c * 256 : c * 256 + 256, :] = nt(spread, grad_pre).astype(BF16)
    return nn(middle_ref[0, c * 256 : c * 256 + 256, :], grad_pre).astype(BF16), part


def hidden_turn_kernel(wire_ref, middle_ref, out_ref, grads_ref):
    inv_rms = inv_rms_of(wire_ref)
    spread = take_hidden(wire_ref, 0)
    grad_mixed = take_hidden(wire_ref, 72)
    mixed, grad_spread, total = [], [], 0.0
    for c in range(4):
        preact = tn(middle_ref[0, c * 256 : c * 256 + 256, :], spread[c]) * inv_rms
        value, slope = gelu_pair(preact)
        act = value.astype(BF16)
        mixed.append(tn(middle_ref[0, 1024 + c * 256 : 1024 + c * 256 + 256, :], act).astype(BF16))
        grad, part = hidden_backward(
            c, grad_mixed[c], act, preact, slope, inv_rms, spread[c], middle_ref, grads_ref
        )
        grad_spread.append(grad)
        total = total + part
    send_hidden(out_ref, 0, grad_spread)
    send_total(out_ref, 64, total * inv_rms)
    send_hidden(out_ref, 72, mixed)


def hidden_backward_kernel(wire_ref, middle_ref, spread_ref, preact_ref, act_ref, inv_ref, out_ref, grads_ref):
    inv_rms = inv_ref[0:1, :]
    grad_mixed = take_hidden(wire_ref, 0)
    grad_spread, total = [], 0.0
    for c in range(4):
        preact = preact_ref[c]
        _, slope = gelu_pair(preact)
        grad, part = hidden_backward(
            c, grad_mixed[c], act_ref[c], preact, slope, inv_rms, spread_ref[c], middle_ref, grads_ref
        )
        grad_spread.append(grad)
        total = total + part
    send_hidden(out_ref, 0, grad_spread)
    send_total(out_ref, 64, total * inv_rms)


def back_through(wire_ref, stream, grad, first_ref, gain_ref, first_grad_ref, gain_grad_ref, section_ref):
    grad_spread = take_features(wire_ref, 0)
    total = take_total(wire_ref, 64)
    gain = gain_column(gain_ref)
    scaled = (stream * gain).astype(BF16)
    norms = []
    for i in range(2):
        part = nt(scaled[i * 128 : i * 128 + 128], grad_spread[i]).astype(BF16)
        for h in range(2):
            first_grad_ref[h * 256 + i * 128 : h * 256 + i * 128 + 128, :] = part[:, h * 256 : h * 256 + 256]
        norms.append(nn(first_of(first_ref, i), grad_spread[i]))
    grad_norm = rows(norms)
    gain_part = jnp.sum(grad_norm * stream, axis=1, keepdims=True)
    gain_row = lanes([jnp.broadcast_to(gain_part[i * 128 : i * 128 + 128], (128, 128)).T[0:1] for i in range(2)])
    high = gain_row.astype(BF16).astype(F32)
    gain_grad_ref[...] = rows([high, gain_row - high, jnp.zeros((14, 256), F32)]).astype(BF16)
    result = grad.astype(F32) + grad_norm * gain - stream * (total / 8192.0)
    section_ref[...] = result.T.astype(BF16)
    return result.astype(BF16)


def fourth_grad(fourth_grad_ref, mixed, grad):
    for i in range(2):
        fourth_grad_ref[:, i * 128 : i * 128 + 128] = nt(mixed[i], grad[i * 128 : i * 128 + 128]).astype(BF16)


def features_turn_kernel(
    wire_ref, stream_ref, grad_ref, first_ref, gain_ref, last_fourth_ref, fourth_ref, mixed_ref,
    out_ref, next_ref, first_grad_ref, gain_grad_ref, section_grad_ref, fourth_grad_ref,
    section_ref, last_fourth_grad_ref,
):
    stream = stream_ref[...].astype(F32)
    grad = grad_ref[...]
    result = back_through(
        wire_ref, stream, grad, first_ref, gain_ref, first_grad_ref, gain_grad_ref, section_grad_ref
    )
    next_ref[...] = result
    send_grad(out_ref, 0, result, fourth_ref)
    fourth_grad(fourth_grad_ref, [mixed_ref[0], mixed_ref[1]], result)
    mixed = take_features(wire_ref, 72)
    section_ref[...] = leave_layer(stream, mixed, last_fourth_ref).astype(F32).T.astype(BF16)
    fourth_grad(last_fourth_grad_ref, mixed, grad)


def features_backward_kernel(
    wire_ref, stream_ref, grad_ref, first_ref, gain_ref, fourth_ref, mixed_ref,
    out_ref, next_ref, first_grad_ref, gain_grad_ref, section_grad_ref, fourth_grad_ref,
):
    result = back_through(
        wire_ref, stream_ref[...].astype(F32), grad_ref[...], first_ref, gain_ref,
        first_grad_ref, gain_grad_ref, section_grad_ref,
    )
    next_ref[...] = result
    send_grad(out_ref, 0, result, fourth_ref)
    fourth_grad(fourth_grad_ref, [mixed_ref[0], mixed_ref[1]], result)


def features_end_kernel(
    wire_ref, stream_ref, grad_ref, first_ref, gain_ref, first_grad_ref, gain_grad_ref, section_grad_ref
):
    back_through(
        wire_ref, stream_ref[...].astype(F32), grad_ref[...], first_ref, gain_ref,
        first_grad_ref, gain_grad_ref, section_grad_ref,
    )


def final_kernel(got_ref, second_ref, third_ref, first_ref, fourth_ref, gain_ref, out_ref, grad_ref):
    def total(start, size):
        return sum(got_ref[q, start : start + size, :].astype(F32) for q in range(4))

    for c in range(4):
        second_ref[0, c] = total(c * 256, 256)
        third_ref[0, c] = total(1024 + c * 256, 256)
    for i in range(2):
        for h in range(2):
            first_ref[0, i, :, h * 256 : h * 256 + 256] = total(ROWS_MID + h * 256 + i * 128, 128)
    both = total(ROWS_MID + ROWS_OUT, ROWS_OUT)
    fourth_ref[0, 0], fourth_ref[0, 1] = both[:, :128], both[:, 128:]
    start = ROWS_MID + 2 * ROWS_OUT
    for q in range(4):
        out_ref[0, 2 * q : 2 * q + 2] = got_ref[q, start : start + 256, :].reshape(2, 128, 256)
        grad_ref[0, 2 * q : 2 * q + 2] = got_ref[q, start + 256 : start + 512, :].reshape(2, 128, 256)
    gain = total(start + 512, 16)
    gain_ref[...] = gain[0:1] + gain[1:2]


def whole(shape):
    return pl.BlockSpec(shape, lambda *_: (0,) * len(shape))


def layer_block(size, layer, index):
    return pl.BlockSpec((1, size, 256), lambda *_: (layer, index, 0))


def middle_block(layer):
    return layer_block(ROWS_MID, layer, 0)


def first_block(layer):
    return layer_block(ROWS_OUT, layer, 4)


def fourth_block(layer):
    return layer_block(ROWS_OUT, layer, 5)


def gain_block(layer):
    return layer_block(16, layer, 192)


PARAMS = pltpu.CompilerParams(vmem_limit_bytes=56 * 1024 * 1024)


def run(kernel, name, specs, outs, *args, scalars=0):
    return pl.pallas_call(
        kernel,
        name=name,
        out_shape=[jax.ShapeDtypeStruct(shape, dtype) for shape, dtype in outs],
        grid_spec=pltpu.PrefetchScalarGridSpec(
            num_scalar_prefetch=scalars,
            grid=(1,),
            in_specs=specs,
            out_specs=[whole(shape) for shape, _ in outs],
        ),
        compiler_params=PARAMS,
    )(*args)


def swap(values, axis):
    return lax.all_to_all(values, axis, 0, 0, tiled=True)


SQUARE = ((256, 256), BF16)
MIXED = ((2, 512, 256), BF16)
HIDDEN = ((4, 256, 256), BF16)


def wire(size):
    return ((32, size, 128), BF16)


def body(inputs, cotangent, norm_gain, first_factor, second_factor, third_factor, fourth_factor):
    slot = lax.axis_index("pipe").astype(jnp.int32).reshape(1)
    tokens = pl.BlockSpec((2, 128, 256), lambda step, slot_ref: (slot_ref[0], 0, 0))
    square = whole((256, 256))
    mixed_spec = whole((2, 512, 256))
    hidden = whole((4, 256, 256))

    def wire_spec(size):
        return whole((32, size, 128))

    own = [first_factor, second_factor, third_factor, fourth_factor, norm_gain]
    (packed,) = run(
        pack_kernel, "pack", [whole(a.shape) for a in own], [((4, 3088, 256), BF16)], *own
    )
    weights = swap(packed, "pipe")

    sent, stream = run(
        start_kernel, "start", [tokens, first_block(0), gain_block(0)], [wire(72), SQUARE],
        slot, inputs, weights, weights, scalars=1,
    )
    streams, mixes, saved, sections = [stream], [], [], []
    for layer in range(3):
        got = swap(sent, "tensor")
        sent, *record = run(
            hidden_forward_kernel, "hidden_forward", [wire_spec(72), middle_block(layer)],
            [wire(64), HIDDEN, ((4, 256, 256), F32), HIDDEN, ((8, 256), F32)], got, weights,
        )
        saved.append(record)
        got = swap(sent, "tensor")
        specs = [wire_spec(64), square, fourth_block(layer), first_block(layer + 1), gain_block(layer + 1)]
        args = [got, streams[layer], weights, weights, weights]
        if layer < 2:
            sent, stream, mixed, section = run(
                between_kernel, "between", specs, [wire(72), SQUARE, MIXED, SQUARE], *args
            )
        else:
            sent, stream, mixed, section, grad = run(
                turn_kernel, "turn", specs + [tokens, fourth_block(3)],
                [wire(136), SQUARE, MIXED, SQUARE, SQUARE], slot, *args, cotangent, weights, scalars=1,
            )
        streams.append(stream)
        mixes.append(mixed)
        sections.append(section)
    got = swap(sent, "tensor")
    middle_grads, first_grads, fourth_grads, gain_grads, section_grads = ([None] * 4 for _ in range(5))
    sent, middle_grads[3] = run(
        hidden_turn_kernel, "hidden_turn", [wire_spec(136), middle_block(3)],
        [wire(136), ((2048, 256), BF16)], got, weights,
    )
    rest = [((512, 256), BF16), ((16, 256), BF16), SQUARE]
    for layer in (3, 2, 1, 0):
        got = swap(sent, "tensor")
        size = 136 if layer == 3 else 72
        specs = [wire_spec(size), square, square, first_block(layer), gain_block(layer)]
        args = [got, streams[layer], grad, weights, weights]
        if layer == 3:
            (sent, grad, first_grads[3], gain_grads[3], section_grads[3], fourth_grads[2], section,
             fourth_grads[3]) = run(
                features_turn_kernel, "features_turn", specs + [fourth_block(3), fourth_block(2), mixed_spec],
                [wire(64), SQUARE] + rest + [((512, 256), BF16), SQUARE, ((512, 256), BF16)],
                *args, weights, weights, mixes[2],
            )
            sections.append(section)
        elif layer > 0:
            (sent, grad, first_grads[layer], gain_grads[layer], section_grads[layer],
             fourth_grads[layer - 1]) = run(
                features_backward_kernel, "features_backward", specs + [fourth_block(layer - 1), mixed_spec],
                [wire(64), SQUARE] + rest + [((512, 256), BF16)], *args, weights, mixes[layer - 1],
            )
        else:
            first_grads[0], gain_grads[0], section_grads[0] = run(
                features_end_kernel, "features_end", specs, rest, *args
            )
        if layer > 0:
            got = swap(sent, "tensor")
            sent, middle_grads[layer - 1] = run(
                hidden_backward_kernel, "hidden_backward",
                [wire_spec(64), middle_block(layer - 1), hidden, hidden, hidden, whole((8, 256))],
                [wire(72), ((2048, 256), BF16)], got, weights, *saved[layer - 1],
            )
    parts = [middle_grads, first_grads, fourth_grads, sections, section_grads, gain_grads]
    whole_sent = jnp.stack([jnp.concatenate([part[layer] for part in parts]) for layer in range(4)])
    got = swap(whole_sent, "pipe")
    outs = [
        (second_factor.shape, F32), (third_factor.shape, F32), (first_factor.shape, F32),
        (fourth_factor.shape, F32), (norm_gain.shape, F32),
        ((1,) + inputs.shape, BF16), ((1,) + inputs.shape, BF16),
    ]
    second, third, first, fourth, gain, section_out, section_grad = run(
        final_kernel, "final", [whole(got.shape)], outs, got
    )
    return section_out, section_grad, gain, first, second, third, fourth


def solution(mesh):
    placed = (
        P(None, None, "tensor"),
        P(None, None, "tensor"),
        P("pipe", "tensor"),
        P("pipe", "tensor", None, None),
        P("pipe", "tensor", None, None),
        P("pipe", "tensor", None, None),
        P("pipe", "tensor", None, None),
    )
    return jax.shard_map(
        body,
        mesh=mesh,
        in_specs=placed,
        out_specs=(
            P("pipe", None, None, "tensor"),
            P("pipe", None, None, "tensor"),
            P("pipe", "tensor"),
            P("pipe", "tensor", None, None),
            P("pipe", "tensor", None, None),
            P("pipe", "tensor", None, None),
            P("pipe", "tensor", None, None),
        ),
        check_vma=False,
    )
```
